32 devices in a mesh: groups: 2 (over y), seq: 4 (over z), tp: 4 (over x, core).
Axes of the slice: x: 2, y: 2, z: 4, core: 2. Of those that a mesh axis runs over, the one named last changes fastest.
Arguments:
- resp_queries: bfloat16 [4096, 8192], P(('groups', 'seq'), 'tp'), parts along dimension 0, may hold values from -300 to 300
- resp_keys: bfloat16 [4096, 1024], P(('groups', 'seq'), 'tp'), parts along dimension 0, may hold values from -4 to 4
- resp_values: bfloat16 [4096, 1024], P(('groups', 'seq'), 'tp'), parts along dimension 0, may hold values from -48 to 48
- prompt_keys: bfloat16 [2048, 1024], P(('groups', 'seq'), 'tp'), parts along dimension 0, may hold values from -4 to 4
- prompt_values: bfloat16 [2048, 1024], P(('groups', 'seq'), 'tp'), parts along dimension 0, may hold values from -48 to 48
- out_weight: bfloat16 [8192, 8192], P('tp', 'seq'), may hold values from -0.0625 to 0.0625
- resp_blocks: int32 [8], P('groups'), parts along dimension 0, may hold values from 1 to 4, 11 in all
Outputs:
- attended: bfloat16 [4096, 8192], P(('groups', 'seq'), 'tp'), parts along dimension 0
The draws below stay inside these ranges and needn't reach their ends.
There are 2 independent parts, one for each index of `groups`. The reference program is written for one: setup_inputs(seed, part) draws one part's arguments, and reference() takes and returns one part's arrays. A program takes and returns all parts, laid end to end along the dimension named above; an argument that names none is the same for every part. Nothing has to cross between parts.
Inputs may be any that keep to these rules, and one draw needn't show every extreme that they name: `resp_blocks`: the lengths sum to 11 blocks and the longest is exactly 4 blocks.
All inputs are finite; a program needn't handle non-finite values.
Results may differ from the reference program's by a relative error of at most 0.017.
Values may be sent and summed in bfloat16 or wider, within the bound.
No kernel may reach another device: no remote copies, remote signals or barrier semaphores. Data moves between devices by JAX's collectives and lax.ppermute only.
A program may use at most 128 MiB of HBM per device.

```python
import math
import jax
import jax.numpy as jnp
import numpy as np
from jax import lax

D = 8192
H = 64
KVH = 8
HD = 128
BLOCK = 128
MAXB = 4
PROMPT = 1024
NRESP = 4
TOTB = 11
N_TP = 4


def prompt_base(key):
    base = jax.random.normal(jax.random.fold_in(key, 11), (PROMPT, KVH * HD), jnp.float32)
    base = jnp.clip(base, -4.0, 4.0)
    return base


def draw_prompt_keys(key, part):
    return prompt_base(key).astype(jnp.bfloat16)


def draw_resp_queries(key, part):
    count = NRESP * MAXB * BLOCK
    values = 1.5 * jax.random.normal(jax.random.fold_in(key, 23), (count, H * HD), jnp.float32)
    values = jnp.clip(values, -9.0, 9.0)
    return values.astype(jnp.bfloat16)


def block_scale(rng, dims, split, smallest, top_value):
    loudness, own = 1.0, jax.random.fold_in(rng, 6)
    for dim, shards_of in split:
        heights = jnp.exp(jax.random.uniform(jax.random.fold_in(own, dim), (shards_of,), jnp.float32, smallest / len(split), top_value / len(split)))
        loudness = loudness * jnp.repeat(heights, dims[dim] // shards_of).reshape([-1 if axis == dim else 1 for axis in range(len(dims))])
    return loudness


def length_profile(amount, total, limit, lean):
    loads = [(1 << 20) // math.isqrt(standing ** lean) + 1 for standing in range(2, amount + 1)]
    rest, given = total - limit - (amount - 1), [1] * (amount - 1)
    while rest > 0:
        candidates = [i for i in range(amount - 1) if given[i] < limit]
        pool, left = sum([loads[i] for i in candidates]), rest
        for i in candidates:
            extra = min(limit - given[i], max(1, left * loads[i] // pool), rest)
            given[i] = given[i] + extra
            rest = rest - extra
    return np.array([limit] + given)


def ragged_sizes(rng, number_of, total, reach, skew):
    if number_of == 2:
        one = jax.random.randint(rng, (), max(1, total - reach), min(reach, total - 1) + 1)
        return jnp.stack([one, total - one])
    lengths = jnp.asarray(length_profile(number_of, total, reach, skew), jnp.int32)
    twos = (number_of - 1) // 2
    source_of, receiver = lengths[1:1 + 2 * twos:2], lengths[2:2 + 2 * twos:2]
    slack = jnp.minimum(source_of - 1, reach - receiver)
    shifted = jax.random.randint(jax.random.fold_in(rng, 1), (twos,), 0, 1 << 20) % (slack + 1)
    lengths = lengths.at[1:1 + 2 * twos:2].set(source_of - shifted).at[2:2 + 2 * twos:2].set(receiver + shifted)
    return lengths[jax.random.permutation(jax.random.fold_in(rng, 2), number_of)]


def bell_draw(rng, shape, scale, bound, split=(), kind=jnp.bfloat16):
    loudness = block_scale(rng, shape, split, -0.22, 0.18) if split else 1.0
    drawn = jax.random.normal(rng, shape, jnp.float32) * scale * loudness
    return jnp.minimum(jnp.maximum(drawn, -bound), bound).astype(kind)


def setup_inputs(seed: int = 0, part: int = 0) -> dict:
    seeds = jax.random.split(jax.random.key(seed), 8)
    own_keys = jax.random.split(jax.random.fold_in(seeds[7], part), 8)
    return {
        "resp_queries": draw_resp_queries(jax.random.fold_in(jax.random.fold_in(seeds[7], part), 71), part),
        "resp_keys": bell_draw(own_keys[1], (NRESP * MAXB * BLOCK, KVH * HD), 1.0, 4.0, ((0, 4), (1, 4))),
        "resp_values": bell_draw(own_keys[2], (NRESP * MAXB * BLOCK, KVH * HD), 8.0, 48.0, ((0, 4), (1, 4))),
        "prompt_keys": draw_prompt_keys(jax.random.fold_in(jax.random.fold_in(seeds[7], part), 71), part),
        "prompt_values": bell_draw(own_keys[4], (PROMPT, KVH * HD), 8.0, 48.0, ((0, 4), (1, 4))),
        "out_weight": bell_draw(seeds[5], (H * HD, D), (H * HD) ** -0.5, 0.0625, ((0, 4), (1, 4))),
        "resp_blocks": ragged_sizes(own_keys[6], NRESP, TOTB, MAXB, 1).astype(jnp.int32),
    }


def reference(resp_queries, resp_keys, resp_values, prompt_keys, prompt_values, out_weight, resp_blocks):
    span = MAXB * BLOCK
    group = H // KVH
    scale = HD ** -0.5
    width = H * HD // N_TP
    prompt_k = prompt_keys.astype(jnp.float32)
    prompt_v = prompt_values.astype(jnp.float32)

    def one_response(packed):
        queries, keys, values, blocks = packed
        length = blocks * BLOCK
        position = jnp.arange(span, dtype=jnp.int32)
        all_keys = jnp.concatenate([prompt_k, keys.astype(jnp.float32)], axis=0)
        all_values = jnp.concatenate([prompt_v, values.astype(jnp.float32)], axis=0)
        allowed = jnp.concatenate([jnp.ones((span, PROMPT), dtype=bool), position[None, :] <= position[:, None]], axis=1)
        pieces = []
        for head_group in range(KVH):
            query_part = queries[:, head_group * group * HD:(head_group + 1) * group * HD].astype(jnp.float32).reshape(span, group, HD)
            key_part = all_keys[:, head_group * HD:(head_group + 1) * HD]
            value_part = all_values[:, head_group * HD:(head_group + 1) * HD]
            scores = jnp.einsum('qhd,nd->hqn', query_part, key_part) * scale
            scores = jnp.where(allowed[None], scores, -jnp.inf)
            top = jnp.max(scores, axis=-1, keepdims=True)
            expo = jnp.exp(scores - top)
            total = jnp.sum(expo, axis=-1, keepdims=True)
            rounded = lax.optimization_barrier(expo.astype(jnp.bfloat16)).astype(jnp.float32)
            numer = jnp.einsum('hqn,nd->hqd', rounded, value_part)
            heads = (numer / total).astype(jnp.bfloat16)
            pieces.append(jnp.transpose(heads, (1, 0, 2)).reshape(span, group * HD))
        attn = jnp.concatenate(pieces, axis=1)
        summed = jnp.zeros((span, D), jnp.float32)
        for tensor_index in range(N_TP):
            partial_value = jnp.dot(attn[:, tensor_index * width:(tensor_index + 1) * width], out_weight[tensor_index * width:(tensor_index + 1) * width], preferred_element_type=jnp.float32)
            summed = summed + lax.optimization_barrier(partial_value.astype(jnp.bfloat16)).astype(jnp.float32)
        live = position < length
        return jnp.where(live[:, None], summed, jnp.zeros_like(summed)).astype(jnp.bfloat16)

    result = lax.map(one_response, (resp_queries.reshape(NRESP, span, H * HD), resp_keys.reshape(NRESP, span, KVH * HD), resp_values.reshape(NRESP, span, KVH * HD), resp_blocks))
    return result.reshape(NRESP * span, D)
```

```python
import functools
import math

import jax
import jax.numpy as jnp
from jax import lax
from jax.experimental import pallas as pl
from jax.experimental.pallas import tpu as pltpu
from jax.sharding import PartitionSpec as P

HD = 128
BLOCK = 128
MAXB = 4
SPLIT = 2
GRAN = BLOCK // SPLIT


def attend_kernel(*refs, kv_local, group, pieces, own):
    q_ref = refs[0]
    shared = refs[1 : 1 + pieces]
    key_ref, value_ref, out_ref = refs[1 + pieces :]
    rows = q_ref.shape[0]
    width = kv_local * HD
    factor = HD ** (-0.5) * math.log2(math.e)
    pair = min(group, 2)
    row = lax.broadcasted_iota(jnp.int32, (pair * rows, rows), 0) % rows
    col = lax.broadcasted_iota(jnp.int32, (pair * rows, rows), 1)
    causal = col <= row
    for kv in range(kv_local):
        cols = slice(kv * HD, (kv + 1) * HD)
        vcols = slice(width + kv * HD, width + (kv + 1) * HD)
        keys = jnp.concatenate(
            [piece[:, cols] for piece in shared] + [key_ref[:own, cols]], axis=0
        )
        values = jnp.concatenate(
            [piece[:, vcols] for piece in shared] + [value_ref[:own, cols]], axis=0
        )
        for first in range(0, group, pair):
            heads = [kv * group + first + i for i in range(pair)]
            queries = jnp.concatenate(
                [q_ref[:, h * HD : (h + 1) * HD] for h in heads], axis=0
            )
            scores = lax.dot_general(
                queries, keys, (((1,), (1,)), ((), ())), preferred_element_type=jnp.float32
            )
            split = scores.shape[1] - rows
            scores = jnp.concatenate(
                [scores[:, :split], jnp.where(causal, scores[:, split:], -1e30)], axis=1
            )
            top = jnp.max(scores, axis=1, keepdims=True)
            expo = jnp.exp2((scores - top) * factor)
            total = jnp.sum(expo, axis=1, keepdims=True)
            numer = jnp.dot(
                expo.astype(jnp.bfloat16), values, preferred_element_type=jnp.float32
            )
            result = (numer / total).astype(jnp.bfloat16)
            for i, h in enumerate(heads):
                out_ref[:, h * HD : (h + 1) * HD] = result[i * rows : (i + 1) * rows]


def attend(block, queries, shared, keys, values):
    head_cols = queries.shape[1]
    kv_cols = keys.shape[1]
    own = (block + 1) * BLOCK
    keys_seen = own + sum(p.shape[0] for p in shared)
    body = functools.partial(
        attend_kernel,
        kv_local=kv_cols // HD,
        group=head_cols // kv_cols,
        pieces=len(shared),
        own=own,
    )
    whole = lambda shape: pl.BlockSpec(shape, lambda i: (0, 0))
    return pl.pallas_call(
        body,
        grid=(1,),
        out_shape=jax.ShapeDtypeStruct((BLOCK, head_cols), queries.dtype),
        in_specs=[pl.BlockSpec((BLOCK, head_cols), lambda i: (block, 0))]
        + [whole(p.shape) for p in shared]
        + [whole(keys.shape), whole(values.shape)],
        out_specs=whole((BLOCK, head_cols)),
        cost_estimate=pl.CostEstimate(
            flops=4 * BLOCK * head_cols * keys_seen,
            bytes_accessed=4 * BLOCK * head_cols,
            transcendentals=BLOCK * keys_seen * head_cols // HD,
        ),
        name=f"attend{block}",
    )(queries, *shared, keys, values)


def per_device(
    resp_queries, resp_keys, resp_values, prompt_keys, prompt_values, out_weight, resp_blocks
):
    nseq = lax.axis_size("seq")
    ntp = lax.axis_size("tp")
    here = lax.axis_index("seq")
    lane = lax.axis_index("tp")
    span = MAXB * BLOCK
    resp_local = resp_queries.shape[0] // span
    assert resp_local == 1 and nseq % ntp == 0
    count = nseq
    total = count + 3 * count // 4 + MAXB
    width = out_weight.shape[1]
    piece_cols = width // ntp
    ratio = nseq // ntp
    most = MAXB * SPLIT
    rounds = (total - 1) * SPLIT
    counts = resp_blocks * SPLIT
    mine = lax.dynamic_index_in_dim(resp_blocks, here, keepdims=False)
    ends = jnp.concatenate([jnp.zeros((1,), jnp.int32), jnp.cumsum(counts)])

    prompt = jnp.concatenate([prompt_keys, prompt_values], axis=1)
    shared = [prompt] + [
        lax.ppermute(prompt, "seq", [(s, (s + k) % nseq) for s in range(nseq)])
        for k in range(1, nseq)
    ]

    heads = [attend(b, resp_queries, shared, resp_keys, resp_values) for b in range(MAXB)]
    own = [
        heads[k // SPLIT][(k % SPLIT) * GRAN : (k % SPLIT + 1) * GRAN] for k in range(most)
    ]

    def reduce_tp(partial):
        bit = 1
        while bit < ntp:
            half = partial.shape[1] // 2
            high = (lane // bit) % 2
            keep = lax.dynamic_slice_in_dim(partial, high * half, half, 1)
            send = lax.dynamic_slice_in_dim(partial, (1 - high) * half, half, 1)
            got = lax.ppermute(send, "tp", [(t, t ^ bit) for t in range(ntp)])
            partial = (keep.astype(jnp.float32) + got.astype(jnp.float32)).astype(jnp.bfloat16)
            bit *= 2
        return partial

    def project(rows):
        return jnp.dot(rows, out_weight, preferred_element_type=jnp.float32).astype(jnp.bfloat16)

    own_sums = reduce_tp(project(jnp.concatenate(heads, axis=0)))

    def link_rounds(passed):
        return SPLIT * min(MAXB * passed, total - (nseq - passed))

    own_count = mine * SPLIT
    got_up, got_down, sums_up, sums_down = [], [], [], []

    for k in range(rounds):
        pairs_up = [(s, s + 1) for s in range(nseq - 1) if k < link_rounds(s + 1)]
        pairs_down = [(nseq - 1 - a, nseq - 1 - b) for a, b in pairs_up]
        if k < most:
            send_up = own[k]
            send_down = own[k]
            for i in range(1, MAXB + 1):
                j = k - SPLIT * i
                if j >= 0:
                    send_up = jnp.where(own_count == SPLIT * i, got_up[j], send_up)
                    send_down = jnp.where(own_count == SPLIT * i, got_down[j], send_down)
        else:
            send_up, send_down = got_up[k - most], got_down[k - most]
            for i in range(1, MAXB):
                j = k - SPLIT * i
                send_up = jnp.where(own_count == SPLIT * i, got_up[j], send_up)
                send_down = jnp.where(own_count == SPLIT * i, got_down[j], send_down)
        got_up.append(lax.ppermute(send_up, "seq", pairs_up))
        got_down.append(lax.ppermute(send_down, "seq", pairs_down))
        if k % SPLIT == SPLIT - 1:
            rows = got_up[k - SPLIT + 1 : k + 1] + got_down[k - SPLIT + 1 : k + 1]
            sums = reduce_tp(project(jnp.concatenate(rows, axis=0)))
            sums_up.append(sums[:BLOCK])
            sums_down.append(sums[BLOCK:])

    bounds = sorted({max(1, nseq // 4), max(1, nseq // 2), nseq - 1})
    order = {t: int(format(t, "b").zfill(ntp.bit_length() - 1)[::-1], 2) for t in range(ntp)}
    arrived = [None] * nseq
    low = -1
    for high in bounds:
        upto = min(MAXB * high, total - 1)
        table = jnp.concatenate(
            [own_sums] + sums_up[:upto] + sums_down[:upto]
            + [jnp.zeros((span, piece_cols), jnp.bfloat16)],
            axis=0,
        )
        for k in range(nseq):
            dest = ((here % ratio) * ntp + lane + k) % nseq
            before = span + (ends[here] - ends[jnp.minimum(dest + 1, here)]) * GRAN
            after = span + upto * BLOCK + (ends[jnp.maximum(dest, here + 1)] - ends[here + 1]) * GRAN
            start = jnp.where(dest == here, 0, jnp.where(dest < here, before, after))
            piece = lax.dynamic_slice_in_dim(table, start, span, 0)
            pairs = []
            for s in range(nseq):
                for t in range(ntp):
                    d = ((s % ratio) * ntp + t + k) % nseq
                    if low < abs(d - s) <= high:
                        pairs.append((s * ntp + t, d * ntp + s // ratio))
            if pairs:
                moved = lax.ppermute(piece, ("seq", "tp"), pairs)
                arrived[k] = moved if arrived[k] is None else arrived[k] + moved
        low = high
    stack = jnp.stack(arrived)
    live = (jnp.arange(span) < mine * BLOCK)[:, None]
    columns = []
    for m_high in range(ratio):
        for place in range(ntp):
            t = order[place]
            k = (here - (m_high * ntp + t)) % nseq
            columns.append(lax.dynamic_index_in_dim(stack, k, keepdims=False))
    return jnp.where(live, jnp.concatenate(columns, axis=1), jnp.zeros((), jnp.bfloat16))


def solution(mesh):
    return jax.shard_map(
        per_device,
        mesh=mesh,
        in_specs=(
            P(("groups", "seq"), "tp"),
            P(("groups", "seq"), "tp"),
            P(("groups", "seq"), "tp"),
            P(("groups", "seq"), "tp"),
            P(("groups", "seq"), "tp"),
            P("tp", "seq"),
            P("groups"),
        ),
        out_specs=P(("groups", "seq"), "tp"),
        check_vma=False,
    )
```

```python
import functools
import math

import jax
import jax.numpy as jnp
from jax import lax
from jax.experimental import pallas as pl
from jax.experimental.pallas import tpu as pltpu
from jax.sharding import PartitionSpec as P

HD = 128
BLOCK = 128
MAXB = 4


def attend_kernel(*refs, kv_local, group, pieces, own):
    q_ref = refs[0]
    shared = refs[1 : 1 + pieces]
    key_ref, value_ref = refs[1 + pieces : 3 + pieces]
    out_ref = refs[-1]
    rows = q_ref.shape[0]
    width = kv_local * HD
    factor = HD ** (-0.5) * math.log2(math.e)
    pair = min(group, 2)
    row = lax.broadcasted_iota(jnp.int32, (pair * rows, rows), 0) % rows
    col = lax.broadcasted_iota(jnp.int32, (pair * rows, rows), 1)
    causal = col <= row
    for kv in range(kv_local):
        cols = slice(kv * HD, (kv + 1) * HD)
        vcols = slice(width + kv * HD, width + (kv + 1) * HD)
        keys = jnp.concatenate(
            [piece[:, cols] for piece in shared] + [key_ref[:own, cols]], axis=0
        )
        values = jnp.concatenate(
            [piece[:, vcols] for piece in shared] + [value_ref[:own, cols]], axis=0
        )
        for first in range(0, group, pair):
            heads = [kv * group + first + i for i in range(pair)]
            queries = jnp.concatenate(
                [q_ref[:, h * HD : (h + 1) * HD] for h in heads], axis=0
            )
            scores = lax.dot_general(
                queries, keys, (((1,), (1,)), ((), ())), preferred_element_type=jnp.float32
            )
            split = scores.shape[1] - rows
            scores = jnp.concatenate(
                [scores[:, :split], jnp.where(causal, scores[:, split:], -1e30)], axis=1
            )
            top = jnp.max(scores, axis=1, keepdims=True)
            expo = jnp.exp2((scores - top) * factor)
            total = jnp.sum(expo, axis=1, keepdims=True)
            numer = jnp.dot(
                expo.astype(jnp.bfloat16), values, preferred_element_type=jnp.float32
            )
            result = (numer / total).astype(jnp.bfloat16)
            for i, h in enumerate(heads):
                out_ref[:, h * HD : (h + 1) * HD] = result[i * rows : (i + 1) * rows]


def attend(block, queries, shared, keys, values, before):
    head_cols = queries.shape[1]
    kv_cols = keys.shape[1]
    own = (block + 1) * BLOCK
    keys_seen = own + sum(p.shape[0] for p in shared)
    body = functools.partial(
        attend_kernel,
        kv_local=kv_cols // HD,
        group=head_cols // kv_cols,
        pieces=len(shared),
        own=own,
    )
    whole = lambda shape: pl.BlockSpec(shape, lambda i: (0, 0))
    return pl.pallas_call(
        body,
        grid=(1,),
        out_shape=jax.ShapeDtypeStruct((BLOCK, head_cols), queries.dtype),
        in_specs=[pl.BlockSpec((BLOCK, head_cols), lambda i: (block, 0))]
        + [whole(p.shape) for p in shared]
        + [whole(keys.shape), whole(values.shape)]
        + [pl.BlockSpec(memory_space=pl.ANY)] * (before is not None),
        out_specs=whole((BLOCK, head_cols)),
        cost_estimate=pl.CostEstimate(
            flops=4 * BLOCK * head_cols * keys_seen,
            bytes_accessed=4 * BLOCK * head_cols,
            transcendentals=BLOCK * keys_seen * head_cols // HD,
        ),
        name=f"attend{block}",
    )(queries, *shared, keys, values, *([] if before is None else [before]))


def slots_needed(passed, count, total):
    best = {0: 0}
    for i in range(passed):
        after = {}
        for used, slots in best.items():
            for length in range(1, MAXB + 1):
                lag = max(length, 2) if i else length
                key = used + length
                after[key] = max(after.get(key, 0), slots + lag)
        best = after
    left = count - passed
    return max(v for u, v in best.items() if left <= total - u <= MAXB * left)


def per_device(
    resp_queries, resp_keys, resp_values, prompt_keys, prompt_values, out_weight, resp_blocks
):
    nseq = lax.axis_size("seq")
    ntp = lax.axis_size("tp")
    here = lax.axis_index("seq")
    lane = lax.axis_index("tp")
    side = lane % 2
    span = MAXB * BLOCK
    resp_local = resp_queries.shape[0] // span
    assert resp_local == 1 and nseq % ntp == 0 and ntp % 2 == 0
    total = nseq + 3 * nseq // 4 + MAXB
    width = out_weight.shape[1]
    ratio = nseq // ntp
    nx = ntp // 2
    piece_cols = width // nx
    mine = lax.dynamic_index_in_dim(resp_blocks, here, keepdims=False)
    lags = jnp.maximum(resp_blocks, 2)
    lag = lax.dynamic_index_in_dim(lags, here, keepdims=False)

    def swap(array):
        return lax.ppermute(array, "tp", [(t, t ^ 1) for t in range(ntp)])

    prompt = jnp.concatenate([prompt_keys, prompt_values], axis=1)
    shared = [prompt] + [
        lax.ppermute(prompt, "seq", [(s, (s + k) % nseq) for s in range(nseq)])
        for k in range(1, nseq)
    ]
    weights = (out_weight, swap(out_weight))

    def project(both):
        return sum(
            jnp.dot(both[i], weights[i], preferred_element_type=jnp.float32) for i in range(2)
        ).astype(jnp.bfloat16)

    own, before = [], None
    for b in range(MAXB):
        before = attend(b, resp_queries, shared, resp_keys, resp_values, before)
        own.append(jnp.stack([before, swap(before)]))

    half = MAXB // 2
    low, high = (jnp.concatenate(own[i * half : (i + 1) * half], axis=1) for i in range(2))
    own_part = project(jnp.where(side == 0, low, high))
    home = here // ratio
    same = jnp.where(lane == home, own_part, jnp.zeros((), jnp.bfloat16)).astype(jnp.float32)
    other = jnp.zeros_like(same)
    for k in range(1, ntp):
        pairs = [(s * ntp + ((s // ratio) ^ k), s * ntp + s // ratio) for s in range(nseq)]
        got = lax.ppermute(own_part, ("seq", "tp"), pairs).astype(jnp.float32)
        if k % 2:
            other = other + got
        else:
            same = same + got
    own_sum = jnp.concatenate(
        [jnp.where(side == 0, same, other), jnp.where(side == 0, other, same)], axis=0
    ).astype(jnp.bfloat16)

    def reduce_x(partial):
        bit = 2
        while bit < ntp:
            cols = partial.shape[1] // 2
            upper = (lane // bit) % 2
            keep = lax.dynamic_slice_in_dim(partial, upper * cols, cols, 1)
            send = lax.dynamic_slice_in_dim(partial, (1 - upper) * cols, cols, 1)
            got = lax.ppermute(send, "tp", [(t, t ^ bit) for t in range(ntp)])
            partial = (keep.astype(jnp.float32) + got.astype(jnp.float32)).astype(jnp.bfloat16)
            bit *= 2
        return partial

    links = [slots_needed(s + 1, nseq, total) for s in range(nseq - 1)]
    rounds = max(links)
    got, sums = [], []
    for k in range(rounds):
        send = own[k] if k < MAXB else got[k - MAXB]
        for i in range(2, MAXB + 1 if k < MAXB else MAXB):
            if k >= i:
                send = jnp.where(lag == i, got[k - i], send)
        pairs = []
        for s, need in enumerate(links):
            if k < need:
                for t in range(0, ntp, 2):
                    pairs.append((s * ntp + t, (s + 1) * ntp + t))
                    mirror = nseq - 1 - s
                    pairs.append((mirror * ntp + t + 1, (mirror - 1) * ntp + t + 1))
        got.append(lax.ppermute(send, ("seq", "tp"), pairs))
        sums.append(reduce_x(project(got[k])))

    steps = jnp.arange(nseq)
    places = [int(format(p, "b").zfill(nx.bit_length() - 1)[::-1], 2) if nx > 1 else 0
              for p in range(nx)]
    columns = [[None] * nx for _ in range(ratio)]
    for d in range(1, nseq):
        first, upto = 2 * (d - 1), min(MAXB * d, rounds)
        between = jnp.where(side == 0, (steps > here - d) & (steps < here),
                            (steps < here + d) & (steps > here))
        skip = jnp.sum(jnp.where(between, lags, 0)) - first
        spare = MAXB * d - upto
        table = sums[first:upto] + [jnp.zeros((spare * BLOCK, piece_cols), jnp.bfloat16)] * (spare > 0)
        table = jnp.concatenate(table, axis=0)
        piece = lax.dynamic_slice_in_dim(table, skip * BLOCK, span, 0)
        for place in range(nx):
            x = places[place]
            pairs = []
            for s in range(nseq):
                for t, to in ((2 * x, s - d), (2 * x + 1, s + d)):
                    if 0 <= to < nseq:
                        pairs.append((s * ntp + t, to * ntp + s // ratio))
            moved = lax.ppermute(piece, ("seq", "tp"), pairs)
            for e in range(ratio):
                part = moved
                if ratio > 1:
                    part = jnp.where(jnp.abs(lane * ratio + e - here) == d, moved, 0)
                old = columns[e][place]
                columns[e][place] = part if old is None else old + part
    outs = []
    for e in range(ratio):
        far = jnp.concatenate(columns[e], axis=1)
        outs.append(jnp.where(lane * ratio + e == here, own_sum, far))
    live = (jnp.arange(span) < mine * BLOCK)[:, None]
    return jnp.where(live, jnp.concatenate(outs, axis=1), jnp.zeros((), jnp.bfloat16))


def solution(mesh):
    return jax.shard_map(
        per_device,
        mesh=mesh,
        in_specs=(
            P(("groups", "seq"), "tp"),
            P(("groups", "seq"), "tp"),
            P(("groups", "seq"), "tp"),
            P(("groups", "seq"), "tp"),
            P(("groups", "seq"), "tp"),
            P("tp", "seq"),
            P("groups"),
        ),
        out_specs=P(("groups", "seq"), "tp"),
        check_vma=False,
    )
```

```python
import functools
import math

import jax
import jax.numpy as jnp
from jax import lax
from jax.experimental import pallas as pl
from jax.experimental.pallas import tpu as pltpu
from jax.sharding import PartitionSpec as P

HD = 128
BLOCK = 128
MAXB = 4


def attend_kernel(*refs, kv_local, group, pieces, own):
    q_ref = refs[0]
    shared = refs[1 : 1 + pieces]
    key_ref, value_ref = refs[1 + pieces : 3 + pieces]
    out_ref = refs[-1]
    rows = q_ref.shape[0]
    width = kv_local * HD
    factor = HD ** (-0.5) * math.log2(math.e)
    pair = min(group, 2)
    row = lax.broadcasted_iota(jnp.int32, (pair * rows, rows), 0) % rows
    col = lax.broadcasted_iota(jnp.int32, (pair * rows, rows), 1)
    causal = col <= row
    for kv in range(kv_local):
        cols = slice(kv * HD, (kv + 1) * HD)
        vcols = slice(width + kv * HD, width + (kv + 1) * HD)
        keys = jnp.concatenate(
            [piece[:, cols] for piece in shared] + [key_ref[:own, cols]], axis=0
        )
        values = jnp.concatenate(
            [piece[:, vcols] for piece in shared] + [value_ref[:own, cols]], axis=0
        )
        for first in range(0, group, pair):
            heads = [kv * group + first + i for i in range(pair)]
            queries = jnp.concatenate(
                [q_ref[:, h * HD : (h + 1) * HD] for h in heads], axis=0
            )
            scores = lax.dot_general(
                queries, keys, (((1,), (1,)), ((), ())), preferred_element_type=jnp.float32
            )
            split = scores.shape[1] - rows
            scores = jnp.concatenate(
                [scores[:, :split], jnp.where(causal, scores[:, split:], -1e30)], axis=1
            )
            top = jnp.max(scores, axis=1, keepdims=True)
            expo = jnp.exp2((scores - top) * factor)
            total = jnp.sum(expo, axis=1, keepdims=True)
            numer = jnp.dot(
                expo.astype(jnp.bfloat16), values, preferred_element_type=jnp.float32
            )
            result = (numer / total).astype(jnp.bfloat16)
            for i, h in enumerate(heads):
                out_ref[:, h * HD : (h + 1) * HD] = result[i * rows : (i + 1) * rows]


def attend(block, queries, shared, keys, values, before):
    head_cols = queries.shape[1]
    kv_cols = keys.shape[1]
    own = (block + 1) * BLOCK
    keys_seen = own + sum(p.shape[0] for p in shared)
    body = functools.partial(
        attend_kernel,
        kv_local=kv_cols // HD,
        group=head_cols // kv_cols,
        pieces=len(shared),
        own=own,
    )
    whole = lambda shape: pl.BlockSpec(shape, lambda i: (0, 0))
    return pl.pallas_call(
        body,
        grid=(1,),
        out_shape=jax.ShapeDtypeStruct((BLOCK, head_cols), queries.dtype),
        in_specs=[pl.BlockSpec((BLOCK, head_cols), lambda i: (block, 0))]
        + [whole(p.shape) for p in shared]
        + [whole(keys.shape), whole(values.shape)]
        + [pl.BlockSpec(memory_space=pl.ANY)] * (before is not None),
        out_specs=whole((BLOCK, head_cols)),
        cost_estimate=pl.CostEstimate(
            flops=4 * BLOCK * head_cols * keys_seen,
            bytes_accessed=4 * BLOCK * head_cols,
            transcendentals=BLOCK * keys_seen * head_cols // HD,
        ),
    )(queries, *shared, keys, values, *([] if before is None else [before]))


def slots_needed(passed, count, total):
    best = {0: 0}
    for i in range(passed):
        after = {}
        for used, slots in best.items():
            for length in range(1, MAXB + 1):
                lag = max(length, 2) if i else length
                key = used + length
                after[key] = max(after.get(key, 0), slots + lag)
        best = after
    left = count - passed
    return max(v for u, v in best.items() if left <= total - u <= MAXB * left)


def project_kernel(base_ref, *refs, parts, adds):
    del base_ref
    mine_ref, other_ref = refs[parts : parts + 2]
    out_ref = refs[-1]
    depth = mine_ref.shape[0]
    first = 0
    for x_ref in refs[:parts]:
        rows = slice(first, first + x_ref.shape[0])
        value = jnp.dot(x_ref[:, :depth], mine_ref[...], preferred_element_type=jnp.float32)
        value += jnp.dot(x_ref[:, depth:], other_ref[...], preferred_element_type=jnp.float32)
        if adds:
            value += refs[parts + 2][rows].astype(jnp.float32)
        out_ref[rows] = value.astype(out_ref.dtype)
        first += x_ref.shape[0]


def project(which, xs, weights, arrived=None):
    depth, width = weights[0].shape
    cols = width // 2
    tile = min(cols, 256)
    rows = sum(x.shape[0] for x in xs)
    extra = [] if arrived is None else [arrived]
    weight = pl.BlockSpec((depth, tile), lambda i, base: (0, base[0] + i))
    column = pl.BlockSpec((rows, tile), lambda i, base: (0, i))
    return pl.pallas_call(
        functools.partial(project_kernel, parts=len(xs), adds=len(extra)),
        out_shape=jax.ShapeDtypeStruct((rows, cols), jnp.bfloat16),
        grid_spec=pltpu.PrefetchScalarGridSpec(
            num_scalar_prefetch=1,
            grid=(cols // tile,),
            in_specs=[pl.BlockSpec(x.shape, lambda i, base: (0, 0)) for x in xs]
            + [weight, weight]
            + [column] * len(extra),
            out_specs=column,
        ),
        cost_estimate=pl.CostEstimate(
            flops=4 * rows * depth * cols, bytes_accessed=4 * depth * cols, transcendentals=0
        ),
        name="project",
    )((which * (cols // tile)).reshape(1), *xs, *weights, *extra)


def pick_kernel(which_ref, *refs, options):
    out_ref, sem = refs[-2:]
    first = 0
    for keys, count in options:
        sources = refs[first : first + count]
        first += count
        hit = which_ref[0] == keys[0]
        for key in keys[1:]:
            hit = hit | (which_ref[0] == key)

        @pl.when(hit)
        def _(sources=sources):
            copies, col = [], 0
            for i, source in enumerate(sources):
                cols = source.shape[1]
                target = out_ref.at[:, col : col + cols]
                copies.append(pltpu.make_async_copy(source, target, sem.at[i]))
                col += cols
            for copy in copies:
                copy.start()
            for copy in copies:
                copy.wait()


def pick(which, options):
    arrays = [array for _, group in options for array in group]
    shape = (arrays[0].shape[0], sum(array.shape[1] for array in options[0][1]))
    return pl.pallas_call(
        functools.partial(pick_kernel, options=[(keys, len(group)) for keys, group in options]),
        out_shape=jax.ShapeDtypeStruct(shape, jnp.bfloat16),
        grid=(1,),
        in_specs=[pl.BlockSpec(memory_space=pltpu.SMEM)]
        + [pl.BlockSpec(memory_space=pl.ANY)] * len(arrays),
        out_specs=pl.BlockSpec(shape, lambda i: (0, 0)),
        scratch_shapes=[pltpu.SemaphoreType.DMA((2,))],
        cost_estimate=pl.CostEstimate(
            flops=0, bytes_accessed=4 * shape[0] * shape[1], transcendentals=0
        ),
        name="pick",
    )(which.reshape(1), *arrays)


def window_kernel(skip_ref, *refs, blocks, out_blocks):
    out_ref, sem = refs[-2:]

    def copy(i, j):
        source, row = blocks[i]
        return pltpu.make_async_copy(
            refs[source].at[row : row + BLOCK], out_ref.at[j * BLOCK : (j + 1) * BLOCK], sem.at[j]
        )

    last = len(blocks) - 1
    for j in range(out_blocks):
        index = jnp.minimum(skip_ref[0] + j, last)
        for i in range(len(blocks)):
            pl.when(index == i)(lambda i=i, j=j: copy(i, j).start())
    for j in range(out_blocks):
        copy(0, j).wait()


def window(skip, arrays, first, upto):
    table, base = [], 0
    for n, array in enumerate(arrays):
        for row in range(0, array.shape[0], BLOCK):
            if first <= base < upto:
                table.append((n, row))
            base += 1
    used = sorted({n for n, _ in table})
    blocks = [(used.index(n), row) for n, row in table]
    cols = arrays[0].shape[1]
    return pl.pallas_call(
        functools.partial(window_kernel, blocks=blocks, out_blocks=MAXB),
        out_shape=jax.ShapeDtypeStruct((MAXB * BLOCK, cols), jnp.bfloat16),
        grid=(1,),
        in_specs=[pl.BlockSpec(memory_space=pltpu.SMEM)]
        + [pl.BlockSpec(memory_space=pl.ANY)] * len(used),
        out_specs=pl.BlockSpec((MAXB * BLOCK, cols), lambda i: (0, 0)),
        scratch_shapes=[pltpu.SemaphoreType.DMA((MAXB,))],
        cost_estimate=pl.CostEstimate(
            flops=0, bytes_accessed=4 * MAXB * BLOCK * cols, transcendentals=0
        ),
        name="window",
    )(skip.reshape(1), *[arrays[n] for n in used])


def rounds_of(nseq):
    total = nseq + 3 * nseq // 4 + MAXB
    links = [slots_needed(s + 1, nseq, total) for s in range(nseq - 1)]
    return links, max(links)


def batches_of(rounds):
    ends = list(range(2, rounds - 1, 2)) + [rounds - 1, rounds]
    return [range(a, b) for a, b in zip([0] + ends, ends) if b > a]


def per_device(
    resp_queries, resp_keys, resp_values, prompt_keys, prompt_values, out_weight, resp_blocks
):
    nseq = lax.axis_size("seq")
    ntp = lax.axis_size("tp")
    here = lax.axis_index("seq")
    lane = lax.axis_index("tp")
    side = lane % 2
    span = MAXB * BLOCK
    assert resp_queries.shape[0] == span and nseq % ntp == 0 and ntp % 4 == 0
    ratio = nseq // ntp
    nx = ntp // 2
    mine = lax.dynamic_index_in_dim(resp_blocks, here, keepdims=False)
    lags = jnp.maximum(resp_blocks, 2)
    lag = lax.dynamic_index_in_dim(lags, here, keepdims=False)
    links, rounds = rounds_of(nseq)
    batches = batches_of(rounds)

    def swap(array):
        return lax.ppermute(array, "tp", [(t, t ^ 1) for t in range(ntp)])

    prompt = jnp.concatenate([prompt_keys, prompt_values], axis=1)
    shared = [prompt] + [
        lax.ppermute(prompt, "seq", [(s, (s + k) % nseq) for s in range(nseq)])
        for k in range(1, nseq)
    ]

    upper = (lane // 2) % 2
    weights = (out_weight, swap(out_weight))

    def summed(xs):
        sent = project(1 - upper, xs, weights)
        arrived = lax.ppermute(sent, "tp", [(t, t ^ 2) for t in range(ntp)])
        partial = project(upper, xs, weights, arrived)
        bit = 4
        while bit < ntp:
            cols = partial.shape[1] // 2
            high = (lane // bit) % 2
            keep = lax.dynamic_slice_in_dim(partial, high * cols, cols, 1)
            send = lax.dynamic_slice_in_dim(partial, (1 - high) * cols, cols, 1)
            got = lax.ppermute(send, "tp", [(t, t ^ bit) for t in range(ntp)])
            partial = (keep.astype(jnp.float32) + got.astype(jnp.float32)).astype(jnp.bfloat16)
            bit *= 2
        return partial

    own, before = [], None
    for b in range(MAXB):
        before = attend(b, resp_queries, shared, resp_keys, resp_values, before)
        own.append([before, swap(before)])

    got = []
    for k in range(rounds):
        options = []
        if k < MAXB:
            options.append((list(range(max(k + 1, 2), MAXB + 1)), own[k]))
        for i in range(2, MAXB + 1):
            if k >= i:
                options.append(([i], [got[k - i]]))
        send = pick(lag, options)
        pairs = []
        for s, need in enumerate(links):
            if k < need:
                for t in range(0, ntp, 2):
                    pairs.append((s * ntp + t, (s + 1) * ntp + t))
                    mirror = nseq - 1 - s
                    pairs.append((mirror * ntp + t + 1, (mirror - 1) * ntp + t + 1))
        got.append(lax.ppermute(send, ("seq", "tp"), pairs))

    half = MAXB // 2
    own_rows = [pick(side, [([0], own[i]), ([1], own[i + half])]) for i in range(half)]
    own_part = summed(own_rows)
    home = here // ratio
    parts = [own_part]
    for k in range(1, ntp):
        pairs = [(s * ntp + ((s // ratio) ^ k), s * ntp + s // ratio) for s in range(nseq)]
        parts.append(lax.ppermute(own_part, ("seq", "tp"), pairs))

    places = [int(format(p, "b").zfill(nx.bit_length() - 1)[::-1], 2) for p in range(nx)]

    def from_lane(t):
        value = parts[t]
        for h in range(1, ntp):
            value = jnp.where(home == h, parts[h ^ t], value)
        return value

    own_sum = jnp.concatenate(
        [
            jnp.concatenate([from_lane(2 * x), from_lane(2 * x + 1)], axis=0) for x in places
        ],
        axis=1,
    )

    sums = [summed([got[k] for k in batch]) for batch in batches]

    steps = jnp.arange(nseq)
    columns = [[None] * nx for _ in range(ratio)]
    for d in range(1, nseq):
        first, upto = 2 * (d - 1), min(MAXB * d, rounds)
        between = jnp.where(side == 0, (steps > here - d) & (steps < here),
                            (steps < here + d) & (steps > here))
        skip = jnp.maximum(jnp.sum(jnp.where(between, lags, 0)) - first, 0)
        piece = window(skip, sums, first, upto)
        for place in range(nx):
            x = places[place]
            pairs = []
            for s in range(nseq):
                for t, to in ((2 * x, s - d), (2 * x + 1, s + d)):
                    if 0 <= to < nseq:
                        pairs.append((s * ntp + t, to * ntp + s // ratio))
            moved = lax.ppermute(piece, ("seq", "tp"), pairs)
            for e in range(ratio):
                part = moved
                if ratio > 1:
                    part = jnp.where(jnp.abs(lane * ratio + e - here) == d, moved, 0)
                old = columns[e][place]
                columns[e][place] = part if old is None else old + part
    outs = []
    for e in range(ratio):
        far = jnp.concatenate(columns[e], axis=1)
        outs.append(jnp.where(lane * ratio + e == here, own_sum, far))
    live = (jnp.arange(span) < mine * BLOCK)[:, None]
    return jnp.where(live, jnp.concatenate(outs, axis=1), jnp.zeros((), jnp.bfloat16))


def solution(mesh):
    return jax.shard_map(
        per_device,
        mesh=mesh,
        in_specs=(
            P(("groups", "seq"), "tp"),
            P(("groups", "seq"), "tp"),
            P(("groups", "seq"), "tp"),
            P(("groups", "seq"), "tp"),
            P(("groups", "seq"), "tp"),
            P("tp", "seq"),
            P("groups"),
        ),
        out_specs=P(("groups", "seq"), "tp"),
        check_vma=False,
    )
```

```python
import functools
import math

import jax
import jax.numpy as jnp
from jax import lax
from jax.experimental import pallas as pl
from jax.experimental.pallas import tpu as pltpu
from jax.sharding import PartitionSpec as P

HD = 128
BLOCK = 128
MAXB = 4


def attend_kernel(*refs, kv_local, group, pieces, own):
    q_ref = refs[0]
    shared = refs[1 : 1 + pieces]
    key_ref, value_ref = refs[1 + pieces : 3 + pieces]
    out_ref = refs[-1]
    rows = q_ref.shape[0]
    width = kv_local * HD
    factor = HD ** (-0.5) * math.log2(math.e)
    pair = min(group, 2)
    row = lax.broadcasted_iota(jnp.int32, (pair * rows, rows), 0) % rows
    col = lax.broadcasted_iota(jnp.int32, (pair * rows, rows), 1)
    causal = col <= row
    for kv in range(kv_local):
        cols = slice(kv * HD, (kv + 1) * HD)
        vcols = slice(width + kv * HD, width + (kv + 1) * HD)
        keys = jnp.concatenate(
            [piece[:, cols] for piece in shared] + [key_ref[:own, cols]], axis=0
        )
        values = jnp.concatenate(
            [piece[:, vcols] for piece in shared] + [value_ref[:own, cols]], axis=0
        )
        for first in range(0, group, pair):
            heads = [kv * group + first + i for i in range(pair)]
            queries = jnp.concatenate(
                [q_ref[:, h * HD : (h + 1) * HD] for h in heads], axis=0
            )
            scores = lax.dot_general(
                queries, keys, (((1,), (1,)), ((), ())), preferred_element_type=jnp.float32
            )
            split = scores.shape[1] - rows
            scores = jnp.concatenate(
                [scores[:, :split], jnp.where(causal, scores[:, split:], -1e30)], axis=1
            )
            top = jnp.max(scores, axis=1, keepdims=True)
            expo = jnp.exp2((scores - top) * factor)
            total = jnp.sum(expo, axis=1, keepdims=True)
            numer = jnp.dot(
                expo.astype(jnp.bfloat16), values, preferred_element_type=jnp.float32
            )
            result = (numer / total).astype(jnp.bfloat16)
            for i, h in enumerate(heads):
                out_ref[:, h * HD : (h + 1) * HD] = result[i * rows : (i + 1) * rows]


def attend(block, queries, shared, keys, values, before):
    head_cols = queries.shape[1]
    kv_cols = keys.shape[1]
    own = (block + 1) * BLOCK
    keys_seen = own + sum(p.shape[0] for p in shared)
    body = functools.partial(
        attend_kernel,
        kv_local=kv_cols // HD,
        group=head_cols // kv_cols,
        pieces=len(shared),
        own=own,
    )
    whole = lambda shape: pl.BlockSpec(shape, lambda i: (0, 0))
    return pl.pallas_call(
        body,
        grid=(1,),
        out_shape=jax.ShapeDtypeStruct((BLOCK, head_cols), queries.dtype),
        in_specs=[pl.BlockSpec((BLOCK, head_cols), lambda i: (block, 0))]
        + [whole(p.shape) for p in shared]
        + [whole(keys.shape), whole(values.shape)]
        + [pl.BlockSpec(memory_space=pl.ANY)] * (before is not None),
        out_specs=whole((BLOCK, head_cols)),
        cost_estimate=pl.CostEstimate(
            flops=4 * BLOCK * head_cols * keys_seen,
            bytes_accessed=4 * BLOCK * head_cols,
            transcendentals=BLOCK * keys_seen * head_cols // HD,
        ),
        compiler_params=pltpu.CompilerParams(vmem_limit_bytes=28 << 20),
    )(queries, *shared, keys, values, *([] if before is None else [before]))


def slots_needed(passed, count, total):
    best = {0: 0}
    for i in range(passed):
        after = {}
        for used, slots in best.items():
            for length in range(1, MAXB + 1):
                lag = max(length, 2) if i else length
                key = used + length
                after[key] = max(after.get(key, 0), slots + lag)
        best = after
    left = count - passed
    return max(v for u, v in best.items() if left <= total - u <= MAXB * left)


def project_kernel(base_ref, *refs, parts, adds):
    del base_ref
    mine_ref, other_ref = refs[parts : parts + 2]
    out_ref = refs[-1]
    depth = mine_ref.shape[0]
    first = 0
    for x_ref in refs[:parts]:
        rows = slice(first, first + x_ref.shape[0])
        value = jnp.dot(x_ref[:, :depth], mine_ref[...], preferred_element_type=jnp.float32)
        value += jnp.dot(x_ref[:, depth:], other_ref[...], preferred_element_type=jnp.float32)
        if adds:
            value += refs[parts + 2][rows].astype(jnp.float32)
        out_ref[rows] = value.astype(out_ref.dtype)
        first += x_ref.shape[0]


def project(which, xs, weights, arrived=None):
    depth, width = weights[0].shape
    cols = width // 2
    tile = min(cols, 256)
    rows = sum(x.shape[0] for x in xs)
    extra = [] if arrived is None else [arrived]
    weight = pl.BlockSpec((depth, tile), lambda i, base: (0, base[0] + i))
    column = pl.BlockSpec((rows, tile), lambda i, base: (0, i))
    return pl.pallas_call(
        functools.partial(project_kernel, parts=len(xs), adds=len(extra)),
        out_shape=jax.ShapeDtypeStruct((rows, cols), jnp.bfloat16),
        grid_spec=pltpu.PrefetchScalarGridSpec(
            num_scalar_prefetch=1,
            grid=(cols // tile,),
            in_specs=[pl.BlockSpec(x.shape, lambda i, base: (0, 0)) for x in xs]
            + [weight, weight]
            + [column] * len(extra),
            out_specs=column,
        ),
        cost_estimate=pl.CostEstimate(
            flops=4 * rows * depth * cols, bytes_accessed=4 * depth * cols, transcendentals=0
        ),
        compiler_params=pltpu.CompilerParams(vmem_limit_bytes=20 << 20),
        name="project",
    )((which * (cols // tile)).reshape(1), *xs, *weights, *extra)


def pick_kernel(which_ref, *refs, options):
    out_ref, sem = refs[-2:]
    first = 0
    for keys, count in options:
        sources = refs[first : first + count]
        first += count
        hit = which_ref[0] == keys[0]
        for key in keys[1:]:
            hit = hit | (which_ref[0] == key)

        @pl.when(hit)
        def _(sources=sources):
            copies, col = [], 0
            for i, source in enumerate(sources):
                cols = source.shape[1]
                target = out_ref.at[:, col : col + cols]
                copies.append(pltpu.make_async_copy(source, target, sem.at[i]))
                col += cols
            for copy in copies:
                copy.start()
            for copy in copies:
                copy.wait()


def pick(which, options):
    arrays = [array for _, group in options for array in group]
    shape = (arrays[0].shape[0], sum(array.shape[1] for array in options[0][1]))
    return pl.pallas_call(
        functools.partial(pick_kernel, options=[(keys, len(group)) for keys, group in options]),
        out_shape=jax.ShapeDtypeStruct(shape, jnp.bfloat16),
        grid=(1,),
        in_specs=[pl.BlockSpec(memory_space=pltpu.SMEM)]
        + [pl.BlockSpec(memory_space=pl.ANY)] * len(arrays),
        out_specs=pl.BlockSpec(shape, lambda i: (0, 0)),
        scratch_shapes=[pltpu.SemaphoreType.DMA((2,))],
        cost_estimate=pl.CostEstimate(
            flops=0, bytes_accessed=4 * shape[0] * shape[1], transcendentals=0
        ),
        compiler_params=pltpu.CompilerParams(vmem_limit_bytes=6 << 20),
        name="pick",
    )(which.reshape(1), *arrays)


def window_kernel(skip_ref, *refs, blocks, out_blocks):
    out_ref, sem = refs[-2:]

    def copy(i, j):
        source, row = blocks[i]
        return pltpu.make_async_copy(
            refs[source].at[row : row + BLOCK], out_ref.at[j * BLOCK : (j + 1) * BLOCK], sem.at[j]
        )

    last = len(blocks) - 1
    for j in range(out_blocks):
        index = jnp.minimum(skip_ref[0] + j, last)
        for i in range(len(blocks)):
            pl.when(index == i)(lambda i=i, j=j: copy(i, j).start())
    for j in range(out_blocks):
        copy(0, j).wait()


def window(skip, arrays, first, upto):
    table, base = [], 0
    for n, array in enumerate(arrays):
        for row in range(0, array.shape[0], BLOCK):
            if first <= base < upto:
                table.append((n, row))
            base += 1
    used = sorted({n for n, _ in table})
    blocks = [(used.index(n), row) for n, row in table]
    cols = arrays[0].shape[1]
    return pl.pallas_call(
        functools.partial(window_kernel, blocks=blocks, out_blocks=MAXB),
        out_shape=jax.ShapeDtypeStruct((MAXB * BLOCK, cols), jnp.bfloat16),
        grid=(1,),
        in_specs=[pl.BlockSpec(memory_space=pltpu.SMEM)]
        + [pl.BlockSpec(memory_space=pl.ANY)] * len(used),
        out_specs=pl.BlockSpec((MAXB * BLOCK, cols), lambda i: (0, 0)),
        scratch_shapes=[pltpu.SemaphoreType.DMA((MAXB,))],
        cost_estimate=pl.CostEstimate(
            flops=0, bytes_accessed=4 * MAXB * BLOCK * cols, transcendentals=0
        ),
        compiler_params=pltpu.CompilerParams(vmem_limit_bytes=6 << 20),
        name="window",
    )(skip.reshape(1), *[arrays[n] for n in used])


def finish_kernel(which_ref, live_ref, *refs, options):
    out_ref, sem = refs[-2:]
    zero = jnp.zeros((BLOCK, out_ref.shape[1]), out_ref.dtype)

    def fill(sources, wait):
        for row in range(0, MAXB * BLOCK, BLOCK):

            @pl.when(row < live_ref[0] * BLOCK)
            def _(row=row):
                for i, (n, base, height, to, col) in enumerate(sources):
                    if to <= row < to + height:
                        source = refs[n]
                        copy = pltpu.make_async_copy(
                            source.at[row - to + base : row - to + base + BLOCK],
                            out_ref.at[row : row + BLOCK, col : col + source.shape[1]],
                            sem.at[i, row // BLOCK],
                        )
                        if wait:
                            copy.wait()
                        else:
                            copy.start()

            if not wait:
                @pl.when(row >= live_ref[0] * BLOCK)
                def _(row=row):
                    out_ref[row : row + BLOCK] = zero

    for key, sources in enumerate(options):

        @pl.when(which_ref[0] == key)
        def _(sources=sources):
            fill(sources, False)
            fill(sources, True)


def finish(which, live, arrays, options):
    cols = max(col + arrays[n].shape[1] for n, _, _, _, col in options[0])
    most = max(len(sources) for sources in options)
    return pl.pallas_call(
        functools.partial(finish_kernel, options=options),
        out_shape=jax.ShapeDtypeStruct((MAXB * BLOCK, cols), jnp.bfloat16),
        grid=(1,),
        in_specs=[pl.BlockSpec(memory_space=pltpu.SMEM)] * 2
        + [pl.BlockSpec(memory_space=pl.ANY)] * len(arrays),
        out_specs=pl.BlockSpec((MAXB * BLOCK, cols), lambda i: (0, 0)),
        scratch_shapes=[pltpu.SemaphoreType.DMA((most, MAXB))],
        compiler_params=pltpu.CompilerParams(vmem_limit_bytes=12 << 20),
        name="finish",
    )(which.reshape(1), live.reshape(1), *arrays)


def rounds_of(nseq):
    total = nseq + 3 * nseq // 4 + MAXB
    links = [slots_needed(s + 1, nseq, total) for s in range(nseq - 1)]
    return links, max(links)


def batches_of(rounds):
    ends = list(range(2, rounds - 1, 2)) + [rounds - 1, rounds]
    return [range(a, b) for a, b in zip([0] + ends, ends) if b > a]


def per_device(
    resp_queries, resp_keys, resp_values, prompt_keys, prompt_values, out_weight, resp_blocks
):
    nseq = lax.axis_size("seq")
    ntp = lax.axis_size("tp")
    here = lax.axis_index("seq")
    lane = lax.axis_index("tp")
    side = lane % 2
    span = MAXB * BLOCK
    assert resp_queries.shape[0] == span and nseq % ntp == 0 and ntp % 4 == 0
    width = out_weight.shape[1]
    ratio = nseq // ntp
    nx = ntp // 2
    piece_cols = width // nx
    mine = lax.dynamic_index_in_dim(resp_blocks, here, keepdims=False)
    lags = jnp.maximum(resp_blocks, 2)
    lag = lax.dynamic_index_in_dim(lags, here, keepdims=False)
    links, rounds = rounds_of(nseq)
    batches = batches_of(rounds)

    def swap(array):
        return lax.ppermute(array, "tp", [(t, t ^ 1) for t in range(ntp)])

    prompt = jnp.concatenate([prompt_keys, prompt_values], axis=1)
    shared = [prompt] + [
        lax.ppermute(prompt, "seq", [(s, (s + k) % nseq) for s in range(nseq)])
        for k in range(1, nseq)
    ]

    upper = (lane // 2) % 2
    weights = (out_weight, swap(out_weight))

    def summed(xs):
        sent = project(1 - upper, xs, weights)
        arrived = lax.ppermute(sent, "tp", [(t, t ^ 2) for t in range(ntp)])
        partial = project(upper, xs, weights, arrived)
        bit = 4
        while bit < ntp:
            cols = partial.shape[1] // 2
            high = (lane // bit) % 2
            keep = lax.dynamic_slice_in_dim(partial, high * cols, cols, 1)
            send = lax.dynamic_slice_in_dim(partial, (1 - high) * cols, cols, 1)
            got = lax.ppermute(send, "tp", [(t, t ^ bit) for t in range(ntp)])
            partial = (keep.astype(jnp.float32) + got.astype(jnp.float32)).astype(jnp.bfloat16)
            bit *= 2
        return partial

    own, before = [], None
    for b in range(MAXB):
        before = attend(b, resp_queries, shared, resp_keys, resp_values, before)
        own.append([before, swap(before)])

    got = []
    for k in range(rounds):
        options = []
        if k < MAXB:
            options.append((list(range(max(k + 1, 2), MAXB + 1)), own[k]))
        for i in range(2, MAXB + 1):
            if k >= i:
                options.append(([i], [got[k - i]]))
        send = pick(lag, options)
        pairs = []
        for s, need in enumerate(links):
            if k < need:
                for t in range(0, ntp, 2):
                    pairs.append((s * ntp + t, (s + 1) * ntp + t))
                    mirror = nseq - 1 - s
                    pairs.append((mirror * ntp + t + 1, (mirror - 1) * ntp + t + 1))
        got.append(lax.ppermute(send, ("seq", "tp"), pairs))

    half = MAXB // 2
    own_rows = [pick(side, [([0], own[i]), ([1], own[i + half])]) for i in range(half)]
    own_part = summed(own_rows)
    home = here // ratio
    parts = [own_part]
    for k in range(1, ntp):
        pairs = [(s * ntp + ((s // ratio) ^ k), s * ntp + s // ratio) for s in range(nseq)]
        parts.append(lax.ppermute(own_part, ("seq", "tp"), pairs))

    places = [int(format(p, "b").zfill(nx.bit_length() - 1)[::-1], 2) for p in range(nx)]

    sums = [summed([got[k] for k in batch]) for batch in batches]

    steps = jnp.arange(nseq)
    moved = {}
    for d in range(1, nseq):
        first, upto = 2 * (d - 1), min(MAXB * d, rounds)
        between = jnp.where(side == 0, (steps > here - d) & (steps < here),
                            (steps < here + d) & (steps > here))
        skip = jnp.maximum(jnp.sum(jnp.where(between, lags, 0)) - first, 0)
        piece = window(skip, sums, first, upto)
        for place in range(nx):
            x = places[place]
            pairs = []
            for s in range(nseq):
                for t, to in ((2 * x, s - d), (2 * x + 1, s + d)):
                    if 0 <= to < nseq:
                        pairs.append((s * ntp + t, to * ntp + s // ratio))
            moved[d, place] = lax.ppermute(piece, ("seq", "tp"), pairs)

    arrays = parts + [moved[d, place] for d in range(1, nseq) for place in range(nx)]
    near = [
        [
            (h ^ (2 * places[place] + c), 0, half * BLOCK, c * half * BLOCK, place * piece_cols)
            for place in range(nx)
            for c in range(2)
        ]
        for h in range(ntp)
    ]
    far = [
        [
            (ntp + (d - 1) * nx + place, 0, span, 0, place * piece_cols) for place in range(nx)
        ]
        for d in range(1, nseq)
    ]
    outs = []
    for e in range(ratio):
        apart = jnp.abs(lane * ratio + e - here)
        which = jnp.where(apart == 0, home, ntp - 1 + apart)
        outs.append(finish(which, mine, arrays, near + far))
    return outs[0] if ratio == 1 else jnp.concatenate(outs, axis=1)


def solution(mesh):
    return jax.shard_map(
        per_device,
        mesh=mesh,
        in_specs=(
            P(("groups", "seq"), "tp"),
            P(("groups", "seq"), "tp"),
            P(("groups", "seq"), "tp"),
            P(("groups", "seq"), "tp"),
            P(("groups", "seq"), "tp"),
            P("tp", "seq"),
            P("groups"),
        ),
        out_specs=P(("groups", "seq"), "tp"),
        check_vma=False,
    )
```

```python
import functools
import math

import jax
import jax.numpy as jnp
from jax import lax
from jax.experimental import pallas as pl
from jax.experimental.pallas import tpu as pltpu
from jax.sharding import PartitionSpec as P

HD = 128
BLOCK = 128
MAXB = 4


def attend_kernel(*refs, kv_local, group, pieces, own):
    q_ref = refs[0]
    shared = refs[1 : 1 + pieces]
    key_ref, value_ref = refs[1 + pieces : 3 + pieces]
    out_ref = refs[-1]
    rows = q_ref.shape[0]
    width = kv_local * HD
    factor = HD ** (-0.5) * math.log2(math.e)
    pair = min(group, 2)
    row = lax.broadcasted_iota(jnp.int32, (pair * rows, rows), 0) % rows
    col = lax.broadcasted_iota(jnp.int32, (pair * rows, rows), 1)
    causal = col <= row
    for kv in range(kv_local):
        cols = slice(kv * HD, (kv + 1) * HD)
        vcols = slice(width + kv * HD, width + (kv + 1) * HD)
        keys = jnp.concatenate(
            [piece[:, cols] for piece in shared] + [key_ref[:own, cols]], axis=0
        )
        values = jnp.concatenate(
            [piece[:, vcols] for piece in shared] + [value_ref[:own, cols]], axis=0
        )
        for first in range(0, group, pair):
            heads = [kv * group + first + i for i in range(pair)]
            queries = jnp.concatenate(
                [q_ref[:, h * HD : (h + 1) * HD] for h in heads], axis=0
            )
            scores = lax.dot_general(
                queries, keys, (((1,), (1,)), ((), ())), preferred_element_type=jnp.float32
            )
            split = scores.shape[1] - rows
            scores = jnp.concatenate(
                [scores[:, :split], jnp.where(causal, scores[:, split:], -1e30)], axis=1
            )
            top = jnp.max(scores, axis=1, keepdims=True)
            expo = jnp.exp2((scores - top) * factor)
            total = jnp.sum(expo, axis=1, keepdims=True)
            numer = jnp.dot(
                expo.astype(jnp.bfloat16), values, preferred_element_type=jnp.float32
            )
            result = (numer / total).astype(jnp.bfloat16)
            for i, h in enumerate(heads):
                out_ref[:, h * HD : (h + 1) * HD] = result[i * rows : (i + 1) * rows]


def attend(block, queries, shared, keys, values, before):
    head_cols = queries.shape[1]
    kv_cols = keys.shape[1]
    own = (block + 1) * BLOCK
    keys_seen = own + sum(p.shape[0] for p in shared)
    body = functools.partial(
        attend_kernel,
        kv_local=kv_cols // HD,
        group=head_cols // kv_cols,
        pieces=len(shared),
        own=own,
    )
    whole = lambda shape: pl.BlockSpec(shape, lambda i: (0, 0))
    return pl.pallas_call(
        body,
        grid=(1,),
        out_shape=jax.ShapeDtypeStruct((BLOCK, head_cols), queries.dtype),
        in_specs=[pl.BlockSpec((BLOCK, head_cols), lambda i: (block, 0))]
        + [whole(p.shape) for p in shared]
        + [whole(keys.shape), whole(values.shape)]
        + [pl.BlockSpec(memory_space=pl.ANY)] * (before is not None),
        out_specs=whole((BLOCK, head_cols)),
        cost_estimate=pl.CostEstimate(
            flops=4 * BLOCK * head_cols * keys_seen,
            bytes_accessed=4 * BLOCK * head_cols,
            transcendentals=BLOCK * keys_seen * head_cols // HD,
        ),
        compiler_params=pltpu.CompilerParams(vmem_limit_bytes=28 << 20),
    )(queries, *shared, keys, values, *([] if before is None else [before]))


def slots_needed(passed, count, total):
    best = {0: 0}
    for i in range(passed):
        after = {}
        for used, slots in best.items():
            for length in range(1, MAXB + 1):
                lag = max(length, 2) if i else length
                key = used + length
                after[key] = max(after.get(key, 0), slots + lag)
        best = after
    left = count - passed
    return max(v for u, v in best.items() if left <= total - u <= MAXB * left)


def project(rows, weight):
    return jnp.dot(rows, weight, preferred_element_type=jnp.float32)


def pick_kernel(which_ref, *refs, options):
    out_ref, sem = refs[-2:]
    first = 0
    for keys, count in options:
        sources = refs[first : first + count]
        first += count
        hit = which_ref[0] == keys[0]
        for key in keys[1:]:
            hit = hit | (which_ref[0] == key)

        @pl.when(hit)
        def _(sources=sources):
            copies, col = [], 0
            for i, source in enumerate(sources):
                cols = source.shape[1]
                target = out_ref.at[:, col : col + cols]
                copies.append(pltpu.make_async_copy(source, target, sem.at[i]))
                col += cols
            for copy in copies:
                copy.start()
            for copy in copies:
                copy.wait()


def pick(which, options):
    arrays = [array for _, group in options for array in group]
    shape = (arrays[0].shape[0], sum(array.shape[1] for array in options[0][1]))
    return pl.pallas_call(
        functools.partial(pick_kernel, options=[(keys, len(group)) for keys, group in options]),
        out_shape=jax.ShapeDtypeStruct(shape, jnp.bfloat16),
        grid=(1,),
        in_specs=[pl.BlockSpec(memory_space=pltpu.SMEM)]
        + [pl.BlockSpec(memory_space=pl.ANY)] * len(arrays),
        out_specs=pl.BlockSpec(shape, lambda i: (0, 0)),
        scratch_shapes=[pltpu.SemaphoreType.DMA((2,))],
        cost_estimate=pl.CostEstimate(
            flops=0, bytes_accessed=4 * shape[0] * shape[1], transcendentals=0
        ),
        compiler_params=pltpu.CompilerParams(vmem_limit_bytes=6 << 20),
        name="pick",
    )(which.reshape(1), *arrays)


def window_kernel(skip_ref, *refs, blocks, out_blocks):
    out_ref, sem = refs[-2:]

    def copy(i, j):
        source, row = blocks[i]
        return pltpu.make_async_copy(
            refs[source].at[row : row + BLOCK], out_ref.at[j * BLOCK : (j + 1) * BLOCK], sem.at[j]
        )

    last = len(blocks) - 1
    for j in range(out_blocks):
        index = jnp.minimum(skip_ref[0] + j, last)
        for i in range(len(blocks)):
            pl.when(index == i)(lambda i=i, j=j: copy(i, j).start())
    for j in range(out_blocks):
        copy(0, j).wait()


def window(skip, arrays, first, upto):
    table, base = [], 0
    for n, array in enumerate(arrays):
        for row in range(0, array.shape[0], BLOCK):
            if first <= base < upto:
                table.append((n, row))
            base += 1
    used = sorted({n for n, _ in table})
    blocks = [(used.index(n), row) for n, row in table]
    cols = arrays[0].shape[1]
    return pl.pallas_call(
        functools.partial(window_kernel, blocks=blocks, out_blocks=MAXB),
        out_shape=jax.ShapeDtypeStruct((MAXB * BLOCK, cols), jnp.bfloat16),
        grid=(1,),
        in_specs=[pl.BlockSpec(memory_space=pltpu.SMEM)]
        + [pl.BlockSpec(memory_space=pl.ANY)] * len(used),
        out_specs=pl.BlockSpec((MAXB * BLOCK, cols), lambda i: (0, 0)),
        scratch_shapes=[pltpu.SemaphoreType.DMA((MAXB,))],
        cost_estimate=pl.CostEstimate(
            flops=0, bytes_accessed=4 * MAXB * BLOCK * cols, transcendentals=0
        ),
        compiler_params=pltpu.CompilerParams(vmem_limit_bytes=6 << 20),
        name="window",
    )(skip.reshape(1), *[arrays[n] for n in used])


def finish_kernel(which_ref, live_ref, *refs, options):
    out_ref, sem = refs[-2:]
    zero = jnp.zeros((BLOCK, out_ref.shape[1]), out_ref.dtype)

    def fill(sources, wait):
        for row in range(0, MAXB * BLOCK, BLOCK):

            @pl.when(row < live_ref[0] * BLOCK)
            def _(row=row):
                for i, (n, base, height, to, col) in enumerate(sources):
                    if to <= row < to + height:
                        source = refs[n]
                        copy = pltpu.make_async_copy(
                            source.at[row - to + base : row - to + base + BLOCK],
                            out_ref.at[row : row + BLOCK, col : col + source.shape[1]],
                            sem.at[i, row // BLOCK],
                        )
                        if wait:
                            copy.wait()
                        else:
                            copy.start()

            if not wait:
                @pl.when(row >= live_ref[0] * BLOCK)
                def _(row=row):
                    out_ref[row : row + BLOCK] = zero

    for key, sources in enumerate(options):

        @pl.when(which_ref[0] == key)
        def _(sources=sources):
            fill(sources, False)
            fill(sources, True)


def finish(which, live, arrays, options):
    cols = max(col + arrays[n].shape[1] for n, _, _, _, col in options[0])
    most = max(len(sources) for sources in options)
    return pl.pallas_call(
        functools.partial(finish_kernel, options=options),
        out_shape=jax.ShapeDtypeStruct((MAXB * BLOCK, cols), jnp.bfloat16),
        grid=(1,),
        in_specs=[pl.BlockSpec(memory_space=pltpu.SMEM)] * 2
        + [pl.BlockSpec(memory_space=pl.ANY)] * len(arrays),
        out_specs=pl.BlockSpec((MAXB * BLOCK, cols), lambda i: (0, 0)),
        scratch_shapes=[pltpu.SemaphoreType.DMA((most, MAXB))],
        compiler_params=pltpu.CompilerParams(vmem_limit_bytes=12 << 20),
        name="finish",
    )(which.reshape(1), live.reshape(1), *arrays)


def rounds_of(nseq):
    total = nseq + 3 * nseq // 4 + MAXB
    links = [slots_needed(s + 1, nseq, total) for s in range(nseq - 1)]
    return links, max(links)


def batches_of(rounds):
    ends = list(range(2, rounds - 1, 2)) + [rounds - 1, rounds]
    return [range(a, b) for a, b in zip([0] + ends, ends) if b > a]


def per_device(
    resp_queries, resp_keys, resp_values, prompt_keys, prompt_values, out_weight, resp_blocks
):
    nseq = lax.axis_size("seq")
    ntp = lax.axis_size("tp")
    here = lax.axis_index("seq")
    lane = lax.axis_index("tp")
    side = lane % 2
    span = MAXB * BLOCK
    assert resp_queries.shape[0] == span and nseq % ntp == 0 and ntp % 4 == 0
    width = out_weight.shape[1]
    ratio = nseq // ntp
    nx = ntp // 2
    piece_cols = width // nx
    mine = lax.dynamic_index_in_dim(resp_blocks, here, keepdims=False)
    lags = jnp.maximum(resp_blocks, 2)
    lag = lax.dynamic_index_in_dim(lags, here, keepdims=False)
    links, rounds = rounds_of(nseq)
    batches = batches_of(rounds)

    def swap(array):
        return lax.ppermute(array, "tp", [(t, t ^ 1) for t in range(ntp)])

    prompt = jnp.concatenate([prompt_keys, prompt_values], axis=1)
    shared = [prompt] + [
        lax.ppermute(prompt, "seq", [(s, (s + k) % nseq) for s in range(nseq)])
        for k in range(1, nseq)
    ]

    upper = (lane // 2) % 2
    halves = [
        lax.dynamic_slice_in_dim(out_weight, side_of * (width // 2), width // 2, 1)
        for side_of in (1 - upper, upper)
    ]
    swapped = []
    for part in halves:
        swapped.append(swap(part))
    send_weight, keep_weight = (
        jnp.concatenate(pair, axis=0) for pair in zip(halves, swapped)
    )

    def summed(xs):
        rows = xs[0] if len(xs) == 1 else jnp.concatenate(xs, axis=0)
        sent = project(rows, send_weight).astype(jnp.bfloat16)
        arrived = lax.ppermute(sent, "tp", [(t, t ^ 2) for t in range(ntp)])
        partial = project(rows, keep_weight) + arrived.astype(jnp.float32)
        partial = partial.astype(jnp.bfloat16)
        bit = 4
        while bit < ntp:
            cols = partial.shape[1] // 2
            high = (lane // bit) % 2
            keep = lax.dynamic_slice_in_dim(partial, high * cols, cols, 1)
            send = lax.dynamic_slice_in_dim(partial, (1 - high) * cols, cols, 1)
            got = lax.ppermute(send, "tp", [(t, t ^ bit) for t in range(ntp)])
            partial = (keep.astype(jnp.float32) + got.astype(jnp.float32)).astype(jnp.bfloat16)
            bit *= 2
        return partial

    own, before = [], None
    for b in range(MAXB):
        before = attend(b, resp_queries, shared, resp_keys, resp_values, before)
        own.append([before, swap(before)])

    got = []
    for k in range(rounds):
        options = []
        if k < MAXB:
            options.append((list(range(max(k + 1, 2), MAXB + 1)), own[k]))
        for i in range(2, MAXB + 1):
            if k >= i:
                options.append(([i], [got[k - i]]))
        send = pick(lag, options)
        pairs = []
        for s, need in enumerate(links):
            if k < need:
                for t in range(0, ntp, 2):
                    pairs.append((s * ntp + t, (s + 1) * ntp + t))
                    mirror = nseq - 1 - s
                    pairs.append((mirror * ntp + t + 1, (mirror - 1) * ntp + t + 1))
        got.append(lax.ppermute(send, ("seq", "tp"), pairs))

    half = MAXB // 2
    own_rows = [pick(side, [([0], own[i]), ([1], own[i + half])]) for i in range(half)]
    own_part = summed(own_rows)
    home = here // ratio
    parts = [own_part]
    for k in range(1, ntp):
        pairs = [(s * ntp + ((s // ratio) ^ k), s * ntp + s // ratio) for s in range(nseq)]
        parts.append(lax.ppermute(own_part, ("seq", "tp"), pairs))

    places = [int(format(p, "b").zfill(nx.bit_length() - 1)[::-1], 2) for p in range(nx)]

    sums = [summed([got[k] for k in batch]) for batch in batches]

    steps = jnp.arange(nseq)
    moved = {}
    for d in range(1, nseq):
        first, upto = 2 * (d - 1), min(MAXB * d, rounds)
        between = jnp.where(side == 0, (steps > here - d) & (steps < here),
                            (steps < here + d) & (steps > here))
        skip = jnp.maximum(jnp.sum(jnp.where(between, lags, 0)) - first, 0)
        piece = window(skip, sums, first, upto)
        for place in range(nx):
            x = places[place]
            pairs = []
            for s in range(nseq):
                for t, to in ((2 * x, s - d), (2 * x + 1, s + d)):
                    if 0 <= to < nseq:
                        pairs.append((s * ntp + t, to * ntp + s // ratio))
            moved[d, place] = lax.ppermute(piece, ("seq", "tp"), pairs)

    arrays = parts + [moved[d, place] for d in range(1, nseq) for place in range(nx)]
    near = [
        [
            (h ^ (2 * places[place] + c), 0, half * BLOCK, c * half * BLOCK, place * piece_cols)
            for place in range(nx)
            for c in range(2)
        ]
        for h in range(ntp)
    ]
    far = [
        [
            (ntp + (d - 1) * nx + place, 0, span, 0, place * piece_cols) for place in range(nx)
        ]
        for d in range(1, nseq)
    ]
    outs = []
    for e in range(ratio):
        apart = jnp.abs(lane * ratio + e - here)
        which = jnp.where(apart == 0, home, ntp - 1 + apart)
        outs.append(finish(which, mine, arrays, near + far))
    return outs[0] if ratio == 1 else jnp.concatenate(outs, axis=1)


def solution(mesh):
    return jax.shard_map(
        per_device,
        mesh=mesh,
        in_specs=(
            P(("groups", "seq"), "tp"),
            P(("groups", "seq"), "tp"),
            P(("groups", "seq"), "tp"),
            P(("groups", "seq"), "tp"),
            P(("groups", "seq"), "tp"),
            P("tp", "seq"),
            P("groups"),
        ),
        out_specs=P(("groups", "seq"), "tp"),
        check_vma=False,
    )
```
